32 devices in a mesh: groups: 2 (over y), ctx: 8 (over z, x), kvh: 2 (over core).
Axes of the slice: x: 2, y: 2, z: 4, core: 2. Of those that a mesh axis runs over, the one named last changes fastest.
Arguments:
- queries: bfloat16 [2048, 4, 8, 128], P(('groups', 'ctx'), 'kvh'), parts along dimension 0, may hold values from -120 to 120
- keys: bfloat16 [2048, 4, 128], P(('groups', 'ctx'), 'kvh'), parts along dimension 0, may hold values from -8 to 8
- values: bfloat16 [2048, 4, 128], P(('groups', 'ctx'), 'kvh'), parts along dimension 0, may hold values from -6 to 6
- seq_lengths: int32 [8], P('groups'), parts along dimension 0, may hold values from 1 to 768, 1024 in all
Outputs:
- attended: bfloat16 [2048, 4, 8, 128], P(('groups', 'ctx'), 'kvh'), parts along dimension 0
The draws below stay inside these ranges and needn't reach their ends.
There are 2 independent parts, one for each index of `groups`. The reference program is written for one: setup_inputs(seed, part) draws one part's arguments, and reference() takes and returns one part's arrays. A program takes and returns all parts, laid end to end along the dimension named above; each array names one. Nothing has to cross between parts.
Inputs may be any that keep to these rules, and one draw needn't show every extreme that they name: `seq_lengths`: sum to 1024; the longest is exactly 768.
All inputs are finite; a program needn't handle non-finite values.
Results may differ from the reference program's by a relative error of at most 0.005.
Values may be sent and summed in bfloat16 or wider, within the bound.
No kernel may reach another device: no remote copies, remote signals or barrier semaphores. Data moves between devices by JAX's collectives and lax.ppermute only.
A program may use at most 64 MiB of HBM per device.

```python
import math
import jax
import jax.numpy as jnp
import numpy as np
from jax import lax

KVH = 4
GROUP = 8
HD = 128
NSEQ = 4
TOKENS = 1024


def shared_keys(key):
    normals = jnp.clip(jax.random.normal(jax.random.fold_in(key, 11), (TOKENS, KVH, HD), jnp.float32), -4.0, 4.0)
    return normals


def draw_keys(key, part):
    return shared_keys(key).astype(jnp.bfloat16)


def draw_queries(key, part):
    normals = jnp.clip(jax.random.normal(jax.random.fold_in(key, 13), (TOKENS, KVH, GROUP, HD), jnp.float32), -4.0, 4.0)
    return normals.astype(jnp.bfloat16)


def block_scale(stream_key, extent, cuts, low, largest):
    def one(position, shards_of):
        draws = jax.random.uniform(jax.random.fold_in(jax.random.fold_in(stream_key, 6), position), (shards_of,), jnp.float32, low / len(cuts), largest / len(cuts))
        return jnp.repeat(jnp.exp(draws), extent[position] // shards_of).reshape((-1,) + (1,) * (len(extent) - position - 1))

    level = one(*cuts[0])
    for cut in cuts[1:]:
        level = level * one(*cut)
    return level


def length_profile(number_of, total, bound, skew):
    weights = [(1 << 20) // math.isqrt(rank ** skew) + 1 for rank in range(2, number_of + 1)]
    rest, counts = total - bound - (number_of - 1), [1] * (number_of - 1)
    while rest > 0:
        free = [i for i in range(number_of - 1) if counts[i] < bound]
        whole, remaining = sum([weights[i] for i in free]), rest
        for i in free:
            extra = min(bound - counts[i], max(1, remaining * weights[i] // whole), rest)
            counts[i] = counts[i] + extra
            rest = rest - extra
    return np.array([bound] + counts)


def uneven(own_key, count, total, bound, lean):
    if count == 2:
        one = jax.random.randint(own_key, (), max(1, total - bound), min(bound, total - 1) + 1)
        return jnp.stack([one, total - one])
    tallies = jnp.asarray(length_profile(count, total, bound, lean), jnp.int32)
    twos = (count - 1) // 2
    donor, receiver = tallies[1:1 + 2 * twos:2], tallies[2:2 + 2 * twos:2]
    room = jnp.minimum(donor - 1, bound - receiver)
    passed = jax.random.randint(jax.random.fold_in(own_key, 1), (twos,), 0, 1 << 20) % (room + 1)
    tallies = tallies.at[1:1 + 2 * twos:2].set(donor - passed).at[2:2 + 2 * twos:2].set(receiver + passed)
    return tallies[jax.random.permutation(jax.random.fold_in(own_key, 2), count)]


def gaussian(rng, dims, spread, most, shards=(), kind=jnp.bfloat16):
    values = jax.random.normal(rng, dims, jnp.float32) * spread
    if len(shards) > 0:
        values = block_scale(rng, dims, shards, -0.22, 0.18) * values
    return jnp.clip(values, min=-most, max=most).astype(kind)


def setup_inputs(seed: int = 0, part: int = 0) -> dict:
    splits = jax.random.split(jax.random.key(seed), 5)
    own_keys = jax.random.split(jax.random.fold_in(splits[4], part), 5)
    queries = draw_queries(jax.random.fold_in(jax.random.fold_in(splits[4], part), 71), part)
    keys = draw_keys(jax.random.fold_in(jax.random.fold_in(splits[4], part), 71), part)
    values = gaussian(own_keys[2], (TOKENS, KVH, HD), 1.0, 6.0, ((0, 8), (1, 2)))
    seq_lengths = uneven(own_keys[3], NSEQ, TOKENS, 3 * TOKENS // 4, 2).astype(jnp.int32)
    return dict(queries=queries, keys=keys, values=values, seq_lengths=seq_lengths)


def reference(queries, keys, values, seq_lengths):
    tokens = queries.shape[0]
    starts = (jnp.cumsum(seq_lengths) - seq_lengths).astype(jnp.int32)
    positions = jnp.arange(tokens, dtype=jnp.int32)
    seq_ids = lax.optimization_barrier(jnp.sum((positions[:, None] >= starts[None, :]).astype(jnp.int32), axis=1))
    key_float = keys.astype(jnp.float32)
    value_float = values.astype(jnp.float32)
    tile_rows = math.gcd(tokens, 256)
    query_tiles = queries.reshape((tokens // tile_rows, tile_rows) + queries.shape[1:])
    tile_first = jnp.arange(tokens // tile_rows, dtype=jnp.int32) * tile_rows
    score_scale = 1.0 / math.sqrt(queries.shape[3])

    def one_tile(inputs):
        query_tile, first_row = inputs
        query_pos = first_row + jnp.arange(tile_rows, dtype=jnp.int32)
        query_seq = lax.dynamic_slice_in_dim(seq_ids, first_row, tile_rows, 0)
        allowed = (seq_ids[None, :] == query_seq[:, None]) & (positions[None, :] <= query_pos[:, None])
        scores = jnp.einsum('rkgd,tkd->rkgt', query_tile.astype(jnp.float32), key_float) * score_scale
        scores = jnp.where(allowed[:, None, None, :], scores, -jnp.inf)
        peak = lax.optimization_barrier(jnp.max(scores, axis=3))
        weights = jnp.exp(scores - peak[..., None])
        denominators = lax.optimization_barrier(jnp.sum(weights, axis=3))
        rounded = weights.astype(jnp.bfloat16).astype(jnp.float32)
        numerators = jnp.einsum('rkgt,tkd->rkgd', rounded, value_float)
        return (numerators / denominators[..., None]).astype(jnp.bfloat16)
    result = lax.map(one_tile, (query_tiles, tile_first))
    return result.reshape(queries.shape)
```

```python
import functools
import math

import jax
import jax.numpy as jnp
from jax import lax
from jax.experimental import pallas as pl
from jax.experimental.pallas import tpu as pltpu
from jax.sharding import PartitionSpec as P

MASKED = -1e30
ROW_TILE = 512


def key_bias(lengths, own, block, rows):
    key_pos = block * rows + lax.broadcasted_iota(jnp.int32, (rows, rows), 0)
    query_pos = own * rows + lax.broadcasted_iota(jnp.int32, (rows, rows), 1)
    low = jnp.zeros((rows, rows), jnp.int32)
    start = jnp.int32(0)
    for n in range(lengths.shape[0]):
        low = jnp.where(query_pos >= start, start, low)
        start = start + lengths[n]
    allowed = (key_pos >= low) & (key_pos <= query_pos)
    return jnp.where(allowed, 0.0, MASKED).astype(jnp.bfloat16)


def attend_tile(query, selector, keys, biases, values, scale):
    lhs = jnp.concatenate([query, selector], axis=1)
    rhs = jnp.concatenate([jnp.concatenate([k, b], axis=1) for k, b in zip(keys, biases)], axis=0)
    scores = lax.dot_general(lhs, rhs, (((1,), (1,)), ((), ())), preferred_element_type=jnp.float32)
    peak = jnp.max(scores, axis=1, keepdims=True)
    weights = jnp.exp2((scores - peak) * scale).astype(jnp.bfloat16)
    ones = jnp.ones_like(values[0])
    right = jnp.concatenate([jnp.concatenate([v, ones], axis=1) for v in values], axis=0)
    return jnp.dot(weights, right, preferred_element_type=jnp.float32)


def pieces_kernel(codes, lengths, query_ref, *refs):
    pieces, out_ref = refs[:-1], refs[-1]
    rows, heads, group, size = query_ref.shape
    own = lax.axis_index("ctx")
    biases = [key_bias(lengths, own, own ^ code, rows) for code in codes]
    scale = math.log2(math.e) / math.sqrt(size)
    tile = min(ROW_TILE, rows * group)
    count = tile // group
    query_row = lax.broadcasted_iota(jnp.int32, (tile, rows), 0) // group
    column = lax.broadcasted_iota(jnp.int32, (tile, rows), 1)
    for h in range(heads):
        keys = [p[0, h] for p in pieces]
        values = [p[1, h] for p in pieces]
        for first in range(0, rows, count):
            query = query_ref[first : first + count, h].reshape(tile, size)
            selector = jnp.where(query_row + first == column, 1.0, 0.0).astype(jnp.bfloat16)
            both = attend_tile(query, selector, keys, biases, values, scale)
            result = both[:, :size] / both[:, size:]
            out_ref[first : first + count, h] = result.astype(jnp.bfloat16).reshape(count, group, size)


def attend_pieces(queries, pieces, codes, lengths):
    vmem = pl.BlockSpec(memory_space=pltpu.VMEM)
    return pl.pallas_call(
        functools.partial(pieces_kernel, codes),
        out_shape=jax.ShapeDtypeStruct(queries.shape, jnp.bfloat16),
        in_specs=[pl.BlockSpec(memory_space=pltpu.SMEM), vmem] + [vmem] * len(pieces),
        out_specs=vmem,
        compiler_params=pltpu.CompilerParams(vmem_limit_bytes=48 * 1024 * 1024),
    )(lengths, queries, *pieces)


def exchange(block, far):
    def swap(array, code):
        return lax.ppermute(array, "ctx", [(i, i ^ code) for i in range(8)])

    crossed = swap(block, far)
    near = [swap(block, code) for code in (2, 1, 3)]
    crossed_near = [swap(crossed, code) for code in (2, 1, 3)]
    codes = (0, 2, 1, 3, far, far ^ 2, far ^ 1, far ^ 3)
    return [block, *near, crossed, *crossed_near], codes


def stream_kernel(step, lengths, query_ref, block_ref, out_ref, peak_ref, both_ref):
    rows, _, group, size = query_ref.shape
    own = lax.axis_index("ctx")
    chunk = pl.program_id(1)
    scale = math.log2(math.e) / math.sqrt(size)

    @pl.when(chunk == 0)
    def _():
        peak_ref[...] = jnp.full_like(peak_ref, MASKED)
        both_ref[...] = jnp.zeros_like(both_ref)

    low, start = jnp.int32(0), jnp.int32(0)
    for n in range(lengths.shape[0]):
        low = jnp.where(own * rows >= start, start, low)
        start = start + lengths[n]

    @pl.when((chunk * step <= own) & ((chunk + 1) * step * rows > low))
    def _():
        tile = rows * group
        query_row = lax.broadcasted_iota(jnp.int32, (tile, rows), 0) // group
        column = lax.broadcasted_iota(jnp.int32, (tile, rows), 1)
        selector = jnp.where(query_row == column, 1.0, 0.0).astype(jnp.bfloat16)
        lhs = jnp.concatenate([query_ref[:, 0].reshape(tile, size), selector], axis=1)
        rhs = jnp.concatenate(
            [
                jnp.concatenate([block_ref[b, 0, 0], key_bias(lengths, own, chunk * step + b, rows)], axis=1)
                for b in range(step)
            ],
            axis=0,
        )
        scores = lax.dot_general(lhs, rhs, (((1,), (1,)), ((), ())), preferred_element_type=jnp.float32)
        before = peak_ref[...]
        peak = jnp.maximum(before, jnp.max(scores, axis=1, keepdims=True))
        weights = jnp.exp2((scores - peak[:, :1]) * scale)
        weights = jnp.where(scores > 0.5 * MASKED, weights, 0.0).astype(jnp.bfloat16)
        value = jnp.concatenate([block_ref[b, 1, 0] for b in range(step)], axis=0)
        right = jnp.concatenate([value, jnp.ones_like(value)], axis=1)
        both_ref[...] = both_ref[...] * jnp.exp2((before[:, :1] - peak[:, :1]) * scale) + jnp.dot(
            weights, right, preferred_element_type=jnp.float32
        )
        peak_ref[...] = peak

    @pl.when(chunk == pl.num_programs(1) - 1)
    def _():
        result = both_ref[:, :size] / both_ref[:, size:]
        out_ref[:, 0] = result.astype(jnp.bfloat16).reshape(rows, group, size)


def attend_gathered(queries, blocks, lengths):
    rows, heads, group, size = queries.shape
    count = blocks.shape[0]
    step = math.gcd(count, 4)
    query_spec = pl.BlockSpec((rows, 1, group, size), lambda h, c: (0, h, 0, 0))
    return pl.pallas_call(
        functools.partial(stream_kernel, step),
        grid=(heads, count // step),
        out_shape=jax.ShapeDtypeStruct(queries.shape, jnp.bfloat16),
        in_specs=[
            pl.BlockSpec(memory_space=pltpu.SMEM),
            query_spec,
            pl.BlockSpec((step, 2, 1, rows, size), lambda h, c: (c, 0, h, 0, 0)),
        ],
        out_specs=query_spec,
        scratch_shapes=[
            pltpu.VMEM((rows * group, size), jnp.float32),
            pltpu.VMEM((rows * group, 2 * size), jnp.float32),
        ],
        compiler_params=pltpu.CompilerParams(vmem_limit_bytes=48 * 1024 * 1024),
    )(lengths, queries, blocks)


def on_device(ctx, queries, keys, values, seq_lengths):
    block = jnp.stack([keys, values]).transpose(0, 2, 1, 3)
    if ctx != 8:
        return attend_gathered(queries, lax.all_gather(block, "ctx"), seq_lengths)
    pieces, codes = exchange(block, 6)
    return attend_pieces(queries, pieces, codes, seq_lengths)


def solution(mesh):
    placed = (
        P(("groups", "ctx"), "kvh", None, None),
        P(("groups", "ctx"), "kvh", None),
        P(("groups", "ctx"), "kvh", None),
        P("groups"),
    )
    return jax.shard_map(
        functools.partial(on_device, mesh.shape["ctx"]),
        mesh=mesh,
        in_specs=placed,
        out_specs=P(("groups", "ctx"), "kvh", None, None),
        check_vma=False,
    )
```

```python
import functools
import math

import jax
import jax.numpy as jnp
from jax import lax
from jax.experimental import pallas as pl
from jax.experimental.pallas import tpu as pltpu
from jax.sharding import PartitionSpec as P

MASKED = -1e30
ROW_TILE = 256
HEADROOM = 60.0


def key_bias(lengths, own, block, rows):
    key_pos = block * rows + lax.broadcasted_iota(jnp.int32, (rows, rows), 0)
    query_pos = own * rows + lax.broadcasted_iota(jnp.int32, (rows, rows), 1)
    low = jnp.zeros((rows, rows), jnp.int32)
    start = jnp.int32(0)
    for n in range(lengths.shape[0]):
        low = jnp.where(query_pos >= start, start, low)
        start = start + lengths[n]
    allowed = (key_pos >= low) & (key_pos <= query_pos)
    return jnp.where(allowed, 0.0, MASKED).astype(jnp.bfloat16)


def ready_kernel(codes, lengths_hbm, query_hbm, lhs_ref, bias_ref, lengths, query_ref, semaphores):
    rows, heads, group, size = query_ref.shape
    fetches = [
        pltpu.make_async_copy(lengths_hbm, lengths, semaphores.at[0]),
        pltpu.make_async_copy(query_hbm, query_ref, semaphores.at[1]),
    ]
    for fetch in fetches:
        fetch.start()
    own = lax.axis_index("ctx")
    query_row = lax.broadcasted_iota(jnp.int32, (rows * group, rows), 0) // group
    column = lax.broadcasted_iota(jnp.int32, (rows * group, rows), 1)
    selector = jnp.where(query_row == column, 1.0, 0.0).astype(jnp.bfloat16)
    for h in range(heads):
        lhs_ref[h, :, size:] = selector
    fetches[0].wait()
    for n, code in enumerate(codes):
        bias_ref[n] = key_bias(lengths, own, own ^ code, rows)
    fetches[1].wait()
    for h in range(heads):
        lhs_ref[h, :, :size] = query_ref[:, h].reshape(rows * group, size)


def scores_of(lhs, h, pieces, biases):
    rhs = jnp.concatenate([jnp.concatenate([p[0, h], b], axis=1) for p, b in zip(pieces, biases)], axis=0)
    return lax.dot_general(lhs, rhs, (((1,), (1,)), ((), ())), preferred_element_type=jnp.float32)


def weigh(above, h, pieces):
    weights = jnp.exp2(above).astype(jnp.bfloat16)
    ones = jnp.ones_like(pieces[0][1, h])
    right = jnp.concatenate([jnp.concatenate([p[1, h], ones], axis=1) for p in pieces], axis=0)
    return jnp.dot(weights, right, preferred_element_type=jnp.float32)


class Output:
    def __init__(self, out_ref, stage_ref, semaphores):
        self.out, self.stage, self.semaphores, self.copies = out_ref, stage_ref, semaphores, []

    def put(self, h, first, both):
        _, _, group, size = self.stage.shape
        result = both[:, :size] / both[:, size:]
        queries = pl.ds(first // group, result.shape[0] // group)
        self.stage[queries, h] = result.astype(jnp.bfloat16).reshape(-1, group, size)
        copy = pltpu.make_async_copy(
            self.stage.at[queries, h], self.out.at[queries, h], self.semaphores.at[len(self.copies)]
        )
        copy.start()
        self.copies.append(copy)

    def wait(self):
        for copy in self.copies:
            copy.wait()


def tiles_of(lhs_ref):
    heads, rows, _ = lhs_ref.shape
    tile = min(ROW_TILE, rows)
    return [(h, first, tile) for first in range(0, rows, tile) for h in range(heads)]


def near_kernel(lhs_ref, bias_ref, *refs):
    pieces, (out_ref, peak_ref, both_ref, stage_ref, semaphores) = refs[:-5], refs[-5:]
    size = stage_ref.shape[-1]
    scale = math.log2(math.e) / math.sqrt(size)
    upper = lax.axis_index("ctx") >= 4
    biases = [bias_ref[n] for n in range(len(pieces))]

    @pl.when(upper)
    def _():
        for h, first, tile in tiles_of(lhs_ref):
            scores = scores_of(lhs_ref[h, pl.ds(first, tile)], h, pieces, biases)
            peak = jnp.max(scores, axis=1, keepdims=True)
            peak_ref[h, pl.ds(first, tile)] = jnp.broadcast_to(peak, (tile, size))
            both_ref[h, pl.ds(first, tile)] = weigh((scores - peak) * scale, h, pieces)

    @pl.when(jnp.logical_not(upper))
    def _():
        output = Output(out_ref, stage_ref, semaphores)
        for h, first, tile in tiles_of(lhs_ref):
            scores = scores_of(lhs_ref[h, pl.ds(first, tile)], h, pieces[:4], biases)
            peak = jnp.max(scores, axis=1, keepdims=True)
            output.put(h, first, weigh((scores - peak) * scale, h, pieces[:4]))
        output.wait()


def far_kernel(skip, lhs_ref, bias_ref, _, peak_ref, both_ref, *refs):
    pieces, (out_ref, stage_ref, semaphores) = refs[:-3], refs[-3:]
    size = stage_ref.shape[-1]
    scale = math.log2(math.e) / math.sqrt(size)
    biases = [bias_ref[skip + n] for n in range(len(pieces))]

    @pl.when(lax.axis_index("ctx") >= 4)
    def _():
        output = Output(out_ref, stage_ref, semaphores)
        most = jnp.full((1, 1), MASKED, jnp.float32)
        for h, first, tile in tiles_of(lhs_ref):
            rows = pl.ds(first, tile)
            scores = scores_of(lhs_ref[h, rows], h, pieces, biases)
            before = peak_ref[h, rows]
            above = (scores - jnp.concatenate([before] * len(pieces), axis=1)) * scale
            most = jnp.maximum(most, jnp.max(above, axis=0, keepdims=True))
            output.put(h, first, both_ref[h, rows] + weigh(above, h, pieces))
        output.wait()

        @pl.when(jnp.max(most) > HEADROOM)
        def _():
            output = Output(out_ref, stage_ref, semaphores)
            for h, first, tile in tiles_of(lhs_ref):
                rows = pl.ds(first, tile)
                scores = scores_of(lhs_ref[h, rows], h, pieces, biases)
                before = peak_ref[h, rows]
                peak = jnp.maximum(before, jnp.max(scores, axis=1, keepdims=True))
                fade = jnp.exp2((before - peak) * scale)
                added = weigh((scores - peak[:, :1]) * scale, h, pieces)
                output.put(h, first, both_ref[h, rows] * jnp.concatenate([fade, fade], axis=1) + added)
            output.wait()


VMEM = pl.BlockSpec(memory_space=pltpu.VMEM)
ANY = pl.BlockSpec(memory_space=pl.ANY)
HBM = pl.BlockSpec(memory_space=pltpu.HBM)
PARAMS = pltpu.CompilerParams(vmem_limit_bytes=24 * 1024 * 1024)


def make_ready(queries, codes, lengths):
    rows, heads, group, size = queries.shape
    return pl.pallas_call(
        functools.partial(ready_kernel, codes),
        out_shape=(
            jax.ShapeDtypeStruct((heads, rows * group, 2 * size), jnp.bfloat16),
            jax.ShapeDtypeStruct((len(codes), rows, rows), jnp.bfloat16),
        ),
        in_specs=[HBM, HBM],
        out_specs=(VMEM, VMEM),
        scratch_shapes=[
            pltpu.SMEM(lengths.shape, jnp.int32),
            pltpu.VMEM(queries.shape, jnp.bfloat16),
            pltpu.SemaphoreType.DMA((2,)),
        ],
        compiler_params=PARAMS,
        name="ready",
    )(pltpu.with_memory_space_constraint(lengths, pltpu.HBM), pltpu.with_memory_space_constraint(queries, pltpu.HBM))


def stage_shapes(shape):
    return [pltpu.VMEM(shape, jnp.bfloat16), pltpu.SemaphoreType.DMA((shape[0] * shape[1] * shape[2] // min(ROW_TILE, shape[0] * shape[2]),))]


def attend_near(shape, lhs, bias, pieces):
    rows, heads, group, size = shape
    return pl.pallas_call(
        near_kernel,
        out_shape=(
            jax.ShapeDtypeStruct(shape, jnp.bfloat16),
            jax.ShapeDtypeStruct((heads, rows * group, size), jnp.float32),
            jax.ShapeDtypeStruct((heads, rows * group, 2 * size), jnp.float32),
        ),
        in_specs=[VMEM, VMEM] + [VMEM] * len(pieces),
        out_specs=(ANY, VMEM, VMEM),
        scratch_shapes=stage_shapes(shape),
        compiler_params=PARAMS,
        name="near",
    )(lhs, bias, *pieces)


def attend_far(lhs, bias, skip, state, pieces):
    shape = state[0].shape
    return pl.pallas_call(
        functools.partial(far_kernel, skip),
        out_shape=jax.ShapeDtypeStruct(shape, jnp.bfloat16),
        in_specs=[VMEM, VMEM, ANY, VMEM, VMEM] + [VMEM] * len(pieces),
        out_specs=ANY,
        scratch_shapes=stage_shapes(shape),
        input_output_aliases={2: 0},
        compiler_params=PARAMS,
        name="far",
    )(lhs, bias, *state, *pieces)


def attend_exchanged(queries, block, lengths):
    def swap(array, code):
        return lax.ppermute(array, "ctx", [(i, i ^ code) for i in range(8)])

    crossed = swap(block, 6)
    near = [swap(block, code) for code in (2, 1, 3)]
    lhs, bias = make_ready(queries, (0, 2, 1, 3, 6, 4, 7, 5), lengths)
    crossed, lhs = lax.optimization_barrier((crossed, lhs))
    spread = [swap(crossed, code) for code in (2, 1, 3)]
    state = attend_near(queries.shape, lhs, bias, [block, *near, crossed])
    return attend_far(lhs, bias, 5, state, spread)


def stream_kernel(step, lengths, query_ref, block_ref, out_ref, peak_ref, both_ref):
    rows, _, group, size = query_ref.shape
    own = lax.axis_index("ctx")
    chunk = pl.program_id(1)
    scale = math.log2(math.e) / math.sqrt(size)

    @pl.when(chunk == 0)
    def _():
        peak_ref[...] = jnp.full_like(peak_ref, MASKED)
        both_ref[...] = jnp.zeros_like(both_ref)

    low, start = jnp.int32(0), jnp.int32(0)
    for n in range(lengths.shape[0]):
        low = jnp.where(own * rows >= start, start, low)
        start = start + lengths[n]

    @pl.when((chunk * step <= own) & ((chunk + 1) * step * rows > low))
    def _():
        tile = rows * group
        query_row = lax.broadcasted_iota(jnp.int32, (tile, rows), 0) // group
        column = lax.broadcasted_iota(jnp.int32, (tile, rows), 1)
        selector = jnp.where(query_row == column, 1.0, 0.0).astype(jnp.bfloat16)
        lhs = jnp.concatenate([query_ref[:, 0].reshape(tile, size), selector], axis=1)
        rhs = jnp.concatenate(
            [
                jnp.concatenate([block_ref[b, 0, 0], key_bias(lengths, own, chunk * step + b, rows)], axis=1)
                for b in range(step)
            ],
            axis=0,
        )
        scores = lax.dot_general(lhs, rhs, (((1,), (1,)), ((), ())), preferred_element_type=jnp.float32)
        before = peak_ref[...]
        peak = jnp.maximum(before, jnp.max(scores, axis=1, keepdims=True))
        weights = jnp.exp2((scores - peak[:, :1]) * scale)
        weights = jnp.where(scores > 0.5 * MASKED, weights, 0.0).astype(jnp.bfloat16)
        value = jnp.concatenate([block_ref[b, 1, 0] for b in range(step)], axis=0)
        right = jnp.concatenate([value, jnp.ones_like(value)], axis=1)
        both_ref[...] = both_ref[...] * jnp.exp2((before[:, :1] - peak[:, :1]) * scale) + jnp.dot(
            weights, right, preferred_element_type=jnp.float32
        )
        peak_ref[...] = peak

    @pl.when(chunk == pl.num_programs(1) - 1)
    def _():
        result = both_ref[:, :size] / both_ref[:, size:]
        out_ref[:, 0] = result.astype(jnp.bfloat16).reshape(rows, group, size)


def attend_gathered(queries, blocks, lengths):
    rows, heads, group, size = queries.shape
    count = blocks.shape[0]
    step = math.gcd(count, 4)
    query_spec = pl.BlockSpec((rows, 1, group, size), lambda h, c: (0, h, 0, 0))
    return pl.pallas_call(
        functools.partial(stream_kernel, step),
        grid=(heads, count // step),
        out_shape=jax.ShapeDtypeStruct(queries.shape, jnp.bfloat16),
        in_specs=[
            pl.BlockSpec(memory_space=pltpu.SMEM),
            query_spec,
            pl.BlockSpec((step, 2, 1, rows, size), lambda h, c: (c, 0, h, 0, 0)),
        ],
        out_specs=query_spec,
        scratch_shapes=[
            pltpu.VMEM((rows * group, size), jnp.float32),
            pltpu.VMEM((rows * group, 2 * size), jnp.float32),
        ],
        compiler_params=pltpu.CompilerParams(vmem_limit_bytes=48 * 1024 * 1024),
    )(lengths, queries, blocks)


def on_device(ctx, queries, keys, values, seq_lengths):
    block = jnp.stack([keys, values]).transpose(0, 2, 1, 3)
    if ctx != 8:
        return attend_gathered(queries, lax.all_gather(block, "ctx"), seq_lengths)
    return attend_exchanged(queries, block, seq_lengths)


def solution(mesh):
    placed = (
        P(("groups", "ctx"), "kvh", None, None),
        P(("groups", "ctx"), "kvh", None),
        P(("groups", "ctx"), "kvh", None),
        P("groups"),
    )
    return jax.shard_map(
        functools.partial(on_device, mesh.shape["ctx"]),
        mesh=mesh,
        in_specs=placed,
        out_specs=P(("groups", "ctx"), "kvh", None, None),
        check_vma=False,
    )
```

```python
import functools
import math

import jax
import jax.numpy as jnp
from jax import lax
from jax.experimental import pallas as pl
from jax.experimental.pallas import tpu as pltpu
from jax.sharding import PartitionSpec as P

MASKED = -1e30
ROW_TILE = 256
HEADROOM = 60.0
NEAR = (3, 2, 1)
SPREAD = (3, 2, 1)


def key_bias(lengths, own, block, rows):
    key_pos = block * rows + lax.broadcasted_iota(jnp.int32, (rows, rows), 0)
    query_pos = own * rows + lax.broadcasted_iota(jnp.int32, (rows, rows), 1)
    low = jnp.zeros((rows, rows), jnp.int32)
    start = jnp.int32(0)
    for n in range(lengths.shape[0]):
        low = jnp.where(query_pos >= start, start, low)
        start = start + lengths[n]
    allowed = (key_pos >= low) & (key_pos <= query_pos)
    return jnp.where(allowed, 0.0, MASKED).astype(jnp.bfloat16)


def ready_kernel(codes, lengths_hbm, query_hbm, lhs_ref, bias_ref, lengths, query_ref, semaphores):
    rows, heads, group, size = query_ref.shape
    fetches = [
        pltpu.make_async_copy(lengths_hbm, lengths, semaphores.at[0]),
        pltpu.make_async_copy(query_hbm, query_ref, semaphores.at[1]),
    ]
    for fetch in fetches:
        fetch.start()
    own = lax.axis_index("ctx")
    query_row = lax.broadcasted_iota(jnp.int32, (rows * group, rows), 0) // group
    column = lax.broadcasted_iota(jnp.int32, (rows * group, rows), 1)
    selector = jnp.where(query_row == column, 1.0, 0.0).astype(jnp.bfloat16)
    for h in range(heads):
        lhs_ref[h, :, size:] = selector
    fetches[0].wait()
    for n, code in enumerate(codes):
        bias_ref[n] = key_bias(lengths, own, own ^ code, rows)
    fetches[1].wait()
    for h in range(heads):
        lhs_ref[h, :, :size] = query_ref[:, h].reshape(rows * group, size)


def scores_of(lhs, h, pieces, biases):
    rhs = jnp.concatenate([jnp.concatenate([p[0, h], b], axis=1) for p, b in zip(pieces, biases)], axis=0)
    return lax.dot_general(lhs, rhs, (((1,), (1,)), ((), ())), preferred_element_type=jnp.float32)


def weigh(above, h, pieces):
    weights = jnp.exp2(above).astype(jnp.bfloat16)
    ones = jnp.ones_like(pieces[0][1, h])
    right = jnp.concatenate([jnp.concatenate([p[1, h], ones], axis=1) for p in pieces], axis=0)
    return jnp.dot(weights, right, preferred_element_type=jnp.float32)


class State:
    def __init__(self, peak_ref, both_ref):
        self.peak, self.both = peak_ref, both_ref

    def restart(self):
        pass

    def wait(self):
        pass

    def __call__(self, h, first, peak, both):
        rows = pl.ds(first, both.shape[0])
        self.peak[h, rows] = jnp.broadcast_to(peak, (both.shape[0], self.peak.shape[-1]))
        self.both[h, rows] = both


class Output:
    def __init__(self, out_ref, stage_ref, semaphores):
        self.out, self.stage, self.semaphores, self.copies = out_ref, stage_ref, semaphores, []

    def restart(self):
        self.copies = []

    def wait(self):
        for copy in self.copies:
            copy.wait()

    def __call__(self, h, first, peak, both):
        _, _, group, size = self.stage.shape
        result = both[:, :size] / both[:, size:]
        queries = pl.ds(first // group, result.shape[0] // group)
        self.stage[queries, h] = result.astype(jnp.bfloat16).reshape(-1, group, size)
        copy = pltpu.make_async_copy(
            self.stage.at[queries, h], self.out.at[queries, h], self.semaphores.at[len(self.copies)]
        )
        copy.start()
        self.copies.append(copy)


def tiles_of(lhs_ref):
    heads, rows, _ = lhs_ref.shape
    tile = min(ROW_TILE, rows)
    return [(h, first, tile) for first in range(0, rows, tile) for h in range(heads)]


def near_kernel(lhs_ref, bias_ref, *refs):
    pieces, (out_ref, peak_ref, both_ref, stage_ref, semaphores) = refs[:-5], refs[-5:]
    size = stage_ref.shape[-1]
    scale = math.log2(math.e) / math.sqrt(size)
    upper = lax.axis_index("ctx") >= 4
    biases = [bias_ref[n] for n in range(len(pieces))]

    def attend(members, put):
        for h, first, tile in tiles_of(lhs_ref):
            scores = scores_of(lhs_ref[h, pl.ds(first, tile)], h, members, biases)
            peak = jnp.max(scores, axis=1, keepdims=True)
            put(h, first, peak, weigh((scores - peak) * scale, h, members))
        put.wait()

    @pl.when(upper)
    def _():
        attend(pieces, State(peak_ref, both_ref))

    @pl.when(jnp.logical_not(upper))
    def _():
        attend(pieces[:4], Output(out_ref, stage_ref, semaphores))


def fold(lhs_ref, peak_ref, both_ref, pieces, biases, put):
    size = peak_ref.shape[-1]
    scale = math.log2(math.e) / math.sqrt(size)
    most = jnp.full((1, 1), MASKED, jnp.float32)
    for h, first, tile in tiles_of(lhs_ref):
        rows = pl.ds(first, tile)
        before = peak_ref[h, rows]
        scores = scores_of(lhs_ref[h, rows], h, pieces, biases)
        above = (scores - jnp.concatenate([before] * len(pieces), axis=1)) * scale
        most = jnp.maximum(most, jnp.max(above, axis=0, keepdims=True))
        put(h, first, before, both_ref[h, rows] + weigh(above, h, pieces))
    put.wait()

    @pl.when(jnp.max(most) > HEADROOM)
    def _():
        put.restart()
        for h, first, tile in tiles_of(lhs_ref):
            rows = pl.ds(first, tile)
            scores = scores_of(lhs_ref[h, rows], h, pieces, biases)
            before = peak_ref[h, rows]
            peak = jnp.maximum(before, jnp.max(scores, axis=1, keepdims=True))
            fade = jnp.exp2((before - peak) * scale)
            added = weigh((scores - jnp.concatenate([peak] * len(pieces), axis=1)) * scale, h, pieces)
            put(h, first, peak, both_ref[h, rows] * jnp.concatenate([fade, fade], axis=1) + added)
        put.wait()


def middle_kernel(skip, lhs_ref, bias_ref, peak_ref, both_ref, *refs):
    pieces, (peak_out, both_out) = refs[:-2], refs[-2:]
    biases = [bias_ref[skip + n] for n in range(len(pieces))]

    @pl.when(lax.axis_index("ctx") >= 4)
    def _():
        fold(lhs_ref, peak_ref, both_ref, pieces, biases, State(peak_out, both_out))


def far_kernel(skip, lhs_ref, bias_ref, _, peak_ref, both_ref, *refs):
    pieces, (out_ref, stage_ref, semaphores) = refs[:-3], refs[-3:]
    biases = [bias_ref[skip + n] for n in range(len(pieces))]

    @pl.when(lax.axis_index("ctx") >= 4)
    def _():
        fold(lhs_ref, peak_ref, both_ref, pieces, biases, Output(out_ref, stage_ref, semaphores))


VMEM = pl.BlockSpec(memory_space=pltpu.VMEM)
ANY = pl.BlockSpec(memory_space=pl.ANY)
HBM = pl.BlockSpec(memory_space=pltpu.HBM)
PARAMS = pltpu.CompilerParams(vmem_limit_bytes=24 * 1024 * 1024)


def make_ready(queries, codes, lengths):
    rows, heads, group, size = queries.shape
    return pl.pallas_call(
        functools.partial(ready_kernel, codes),
        out_shape=(
            jax.ShapeDtypeStruct((heads, rows * group, 2 * size), jnp.bfloat16),
            jax.ShapeDtypeStruct((len(codes), rows, rows), jnp.bfloat16),
        ),
        in_specs=[HBM, HBM],
        out_specs=(VMEM, VMEM),
        scratch_shapes=[
            pltpu.SMEM(lengths.shape, jnp.int32),
            pltpu.VMEM(queries.shape, jnp.bfloat16),
            pltpu.SemaphoreType.DMA((2,)),
        ],
        compiler_params=PARAMS,
        name="ready",
    )(pltpu.with_memory_space_constraint(lengths, pltpu.HBM), pltpu.with_memory_space_constraint(queries, pltpu.HBM))


def stage_shapes(shape):
    return [pltpu.VMEM(shape, jnp.bfloat16), pltpu.SemaphoreType.DMA((shape[0] * shape[1] * shape[2] // min(ROW_TILE, shape[0] * shape[2]),))]


def attend_near(shape, lhs, bias, pieces):
    rows, heads, group, size = shape
    return pl.pallas_call(
        near_kernel,
        out_shape=(
            jax.ShapeDtypeStruct(shape, jnp.bfloat16),
            jax.ShapeDtypeStruct((heads, rows * group, size), jnp.float32),
            jax.ShapeDtypeStruct((heads, rows * group, 2 * size), jnp.float32),
        ),
        in_specs=[VMEM, VMEM] + [VMEM] * len(pieces),
        out_specs=(ANY, VMEM, VMEM),
        scratch_shapes=stage_shapes(shape),
        compiler_params=PARAMS,
        name="near",
    )(lhs, bias, *pieces)


def attend_middle(lhs, bias, skip, state, pieces):
    out, peak, both = state
    peak, both = pl.pallas_call(
        functools.partial(middle_kernel, skip),
        out_shape=(jax.ShapeDtypeStruct(peak.shape, peak.dtype), jax.ShapeDtypeStruct(both.shape, both.dtype)),
        in_specs=[VMEM] * (4 + len(pieces)),
        out_specs=(VMEM, VMEM),
        compiler_params=PARAMS,
        name="middle",
    )(lhs, bias, peak, both, *pieces)
    return out, peak, both


def attend_far(lhs, bias, skip, state, pieces):
    shape = state[0].shape
    return pl.pallas_call(
        functools.partial(far_kernel, skip),
        out_shape=jax.ShapeDtypeStruct(shape, jnp.bfloat16),
        in_specs=[VMEM, VMEM, ANY, VMEM, VMEM] + [VMEM] * len(pieces),
        out_specs=ANY,
        scratch_shapes=stage_shapes(shape),
        input_output_aliases={2: 0},
        compiler_params=PARAMS,
        name="far",
    )(lhs, bias, *state, *pieces)


def attend_exchanged(queries, block, lengths):
    def swap(array, code, members=range(8)):
        return lax.ppermute(array, "ctx", [(i, i ^ code) for i in members])

    crossed = swap(block, 6)
    near = [swap(block, code) for code in NEAR]
    lhs, bias = make_ready(queries, (0, *NEAR, 6, *[6 ^ code for code in SPREAD]), lengths)
    crossed, lhs = lax.optimization_barrier((crossed, lhs))
    spread = [swap(crossed, code, range(4, 8) if code == 3 else range(8)) for code in SPREAD]
    state = attend_near(queries.shape, lhs, bias, [block, *near, crossed])
    state = attend_middle(lhs, bias, 5, state, spread[:1])
    return attend_far(lhs, bias, 6, state, spread[1:])


def stream_kernel(step, lengths, query_ref, block_ref, out_ref, peak_ref, both_ref):
    rows, _, group, size = query_ref.shape
    own = lax.axis_index("ctx")
    chunk = pl.program_id(1)
    scale = math.log2(math.e) / math.sqrt(size)

    @pl.when(chunk == 0)
    def _():
        peak_ref[...] = jnp.full_like(peak_ref, MASKED)
        both_ref[...] = jnp.zeros_like(both_ref)

    low, start = jnp.int32(0), jnp.int32(0)
    for n in range(lengths.shape[0]):
        low = jnp.where(own * rows >= start, start, low)
        start = start + lengths[n]

    @pl.when((chunk * step <= own) & ((chunk + 1) * step * rows > low))
    def _():
        tile = rows * group
        query_row = lax.broadcasted_iota(jnp.int32, (tile, rows), 0) // group
        column = lax.broadcasted_iota(jnp.int32, (tile, rows), 1)
        selector = jnp.where(query_row == column, 1.0, 0.0).astype(jnp.bfloat16)
        lhs = jnp.concatenate([query_ref[:, 0].reshape(tile, size), selector], axis=1)
        rhs = jnp.concatenate(
            [
                jnp.concatenate([block_ref[b, 0, 0], key_bias(lengths, own, chunk * step + b, rows)], axis=1)
                for b in range(step)
            ],
            axis=0,
        )
        scores = lax.dot_general(lhs, rhs, (((1,), (1,)), ((), ())), preferred_element_type=jnp.float32)
        before = peak_ref[...]
        peak = jnp.maximum(before, jnp.max(scores, axis=1, keepdims=True))
        weights = jnp.exp2((scores - peak[:, :1]) * scale)
        weights = jnp.where(scores > 0.5 * MASKED, weights, 0.0).astype(jnp.bfloat16)
        value = jnp.concatenate([block_ref[b, 1, 0] for b in range(step)], axis=0)
        right = jnp.concatenate([value, jnp.ones_like(value)], axis=1)
        both_ref[...] = both_ref[...] * jnp.exp2((before[:, :1] - peak[:, :1]) * scale) + jnp.dot(
            weights, right, preferred_element_type=jnp.float32
        )
        peak_ref[...] = peak

    @pl.when(chunk == pl.num_programs(1) - 1)
    def _():
        result = both_ref[:, :size] / both_ref[:, size:]
        out_ref[:, 0] = result.astype(jnp.bfloat16).reshape(rows, group, size)


def attend_gathered(queries, blocks, lengths):
    rows, heads, group, size = queries.shape
    count = blocks.shape[0]
    step = math.gcd(count, 4)
    query_spec = pl.BlockSpec((rows, 1, group, size), lambda h, c: (0, h, 0, 0))
    return pl.pallas_call(
        functools.partial(stream_kernel, step),
        grid=(heads, count // step),
        out_shape=jax.ShapeDtypeStruct(queries.shape, jnp.bfloat16),
        in_specs=[
            pl.BlockSpec(memory_space=pltpu.SMEM),
            query_spec,
            pl.BlockSpec((step, 2, 1, rows, size), lambda h, c: (c, 0, h, 0, 0)),
        ],
        out_specs=query_spec,
        scratch_shapes=[
            pltpu.VMEM((rows * group, size), jnp.float32),
            pltpu.VMEM((rows * group, 2 * size), jnp.float32),
        ],
        compiler_params=pltpu.CompilerParams(vmem_limit_bytes=48 * 1024 * 1024),
    )(lengths, queries, blocks)


def on_device(ctx, queries, keys, values, seq_lengths):
    block = jnp.stack([keys, values]).transpose(0, 2, 1, 3)
    if ctx != 8:
        return attend_gathered(queries, lax.all_gather(block, "ctx"), seq_lengths)
    return attend_exchanged(queries, block, seq_lengths)


def solution(mesh):
    placed = (
        P(("groups", "ctx"), "kvh", None, None),
        P(("groups", "ctx"), "kvh", None),
        P(("groups", "ctx"), "kvh", None),
        P("groups"),
    )
    return jax.shard_map(
        functools.partial(on_device, mesh.shape["ctx"]),
        mesh=mesh,
        in_specs=placed,
        out_specs=P(("groups", "ctx"), "kvh", None, None),
        check_vma=False,
    )
```

```python
import functools
import math

import jax
import jax.numpy as jnp
from jax import lax
from jax.experimental import pallas as pl
from jax.experimental.pallas import tpu as pltpu
from jax.sharding import PartitionSpec as P

MASKED = -1e30
ROW_TILE = 256
HEADROOM = 60.0


def key_bias(lengths, own, block, rows):
    key_pos = block * rows + lax.broadcasted_iota(jnp.int32, (rows, rows), 0)
    query_pos = own * rows + lax.broadcasted_iota(jnp.int32, (rows, rows), 1)
    low = jnp.zeros((rows, rows), jnp.int32)
    start = jnp.int32(0)
    for n in range(lengths.shape[0]):
        low = jnp.where(query_pos >= start, start, low)
        start = start + lengths[n]
    allowed = (key_pos >= low) & (key_pos <= query_pos)
    return jnp.where(allowed, 0.0, MASKED).astype(jnp.bfloat16)


def ready_kernel(codes, lengths_hbm, query_hbm, lhs_ref, bias_ref, lengths, query_ref, semaphores):
    rows, heads, group, size = query_ref.shape
    fetches = [
        pltpu.make_async_copy(lengths_hbm, lengths, semaphores.at[0]),
        pltpu.make_async_copy(query_hbm, query_ref, semaphores.at[1]),
    ]
    for fetch in fetches:
        fetch.start()
    own = lax.axis_index("ctx")
    query_row = lax.broadcasted_iota(jnp.int32, (rows * group, rows), 0) // group
    column = lax.broadcasted_iota(jnp.int32, (rows * group, rows), 1)
    selector = jnp.where(query_row == column, 1.0, 0.0).astype(jnp.bfloat16)
    for h in range(heads):
        lhs_ref[h, :, size:] = selector
    fetches[0].wait()
    for n, code in enumerate(codes):
        bias_ref[n] = key_bias(lengths, own, own ^ code, rows)
    fetches[1].wait()
    for h in range(heads):
        lhs_ref[h, :, :size] = query_ref[:, h].reshape(rows * group, size)


def scores_of(lhs, h, pieces, biases):
    rhs = jnp.concatenate([jnp.concatenate([p[0, h], b], axis=1) for p, b in zip(pieces, biases)], axis=0)
    return lax.dot_general(lhs, rhs, (((1,), (1,)), ((), ())), preferred_element_type=jnp.float32)


def weigh(above, h, pieces):
    weights = jnp.exp2(above).astype(jnp.bfloat16)
    ones = jnp.ones_like(pieces[0][1, h])
    right = jnp.concatenate([jnp.concatenate([p[1, h], ones], axis=1) for p in pieces], axis=0)
    return jnp.dot(weights, right, preferred_element_type=jnp.float32)


class State:
    def __init__(self, peak_ref, both_ref):
        self.peak, self.both = peak_ref, both_ref

    def restart(self):
        pass

    def wait(self):
        pass

    def __call__(self, h, first, peak, both):
        rows = pl.ds(first, both.shape[0])
        self.peak[h, rows] = jnp.broadcast_to(peak, (both.shape[0], self.peak.shape[-1]))
        self.both[h, rows] = both


class Output:
    def __init__(self, out_ref, stage_ref, semaphores):
        self.out, self.stage, self.semaphores, self.copies = out_ref, stage_ref, semaphores, []

    def restart(self):
        self.copies = []

    def wait(self):
        for copy in self.copies:
            copy.wait()

    def __call__(self, h, first, peak, both):
        _, _, group, size = self.stage.shape
        result = both[:, :size] / both[:, size:]
        queries = pl.ds(first // group, result.shape[0] // group)
        self.stage[queries, h] = result.astype(jnp.bfloat16).reshape(-1, group, size)
        copy = pltpu.make_async_copy(
            self.stage.at[queries, h], self.out.at[queries, h], self.semaphores.at[len(self.copies)]
        )
        copy.start()
        self.copies.append(copy)


def tiles_of(lhs_ref):
    heads, rows, _ = lhs_ref.shape
    tile = min(ROW_TILE, rows)
    return [(h, first, tile) for first in range(0, rows, tile) for h in range(heads)]


def near_kernel(lhs_ref, bias_ref, *refs):
    pieces, (out_ref, peak_ref, both_ref, stage_ref, semaphores) = refs[:-5], refs[-5:]
    size = stage_ref.shape[-1]
    scale = math.log2(math.e) / math.sqrt(size)
    upper = lax.axis_index("ctx") >= 4
    biases = [bias_ref[n] for n in range(len(pieces))]

    def attend(members, put):
        for h, first, tile in tiles_of(lhs_ref):
            scores = scores_of(lhs_ref[h, pl.ds(first, tile)], h, members, biases)
            peak = jnp.max(scores, axis=1, keepdims=True)
            put(h, first, peak, weigh((scores - peak) * scale, h, members))
        put.wait()

    @pl.when(upper)
    def _():
        attend(pieces, State(peak_ref, both_ref))

    @pl.when(jnp.logical_not(upper))
    def _():
        attend(pieces[:4], Output(out_ref, stage_ref, semaphores))


def fold(lhs_ref, peak_ref, both_ref, pieces, biases, put):
    size = peak_ref.shape[-1]
    scale = math.log2(math.e) / math.sqrt(size)
    most = jnp.full((1, 1), MASKED, jnp.float32)
    for h, first, tile in tiles_of(lhs_ref):
        rows = pl.ds(first, tile)
        before = peak_ref[h, rows]
        scores = scores_of(lhs_ref[h, rows], h, pieces, biases)
        above = (scores - jnp.concatenate([before] * len(pieces), axis=1)) * scale
        most = jnp.maximum(most, jnp.max(above, axis=0, keepdims=True))
        put(h, first, before, both_ref[h, rows] + weigh(above, h, pieces))
    put.wait()

    @pl.when(jnp.max(most) > HEADROOM)
    def _():
        put.restart()
        for h, first, tile in tiles_of(lhs_ref):
            rows = pl.ds(first, tile)
            scores = scores_of(lhs_ref[h, rows], h, pieces, biases)
            before = peak_ref[h, rows]
            peak = jnp.maximum(before, jnp.max(scores, axis=1, keepdims=True))
            fade = jnp.exp2((before - peak) * scale)
            added = weigh((scores - jnp.concatenate([peak] * len(pieces), axis=1)) * scale, h, pieces)
            put(h, first, peak, both_ref[h, rows] * jnp.concatenate([fade, fade], axis=1) + added)
        put.wait()


def middle_kernel(skip, lhs_ref, bias_ref, peak_ref, both_ref, *refs):
    pieces, (peak_out, both_out) = refs[:-2], refs[-2:]
    biases = [bias_ref[skip + n] for n in range(len(pieces))]

    @pl.when(lax.axis_index("ctx") >= 4)
    def _():
        fold(lhs_ref, peak_ref, both_ref, pieces, biases, State(peak_out, both_out))


def far_kernel(skip, lhs_ref, bias_ref, _, peak_ref, both_ref, *refs):
    pieces, (out_ref, stage_ref, semaphores) = refs[:-3], refs[-3:]
    biases = [bias_ref[skip + n] for n in range(len(pieces))]

    @pl.when(lax.axis_index("ctx") >= 4)
    def _():
        fold(lhs_ref, peak_ref, both_ref, pieces, biases, Output(out_ref, stage_ref, semaphores))


VMEM = pl.BlockSpec(memory_space=pltpu.VMEM)
ANY = pl.BlockSpec(memory_space=pl.ANY)
HBM = pl.BlockSpec(memory_space=pltpu.HBM)
PARAMS = pltpu.CompilerParams(vmem_limit_bytes=24 * 1024 * 1024)


def make_ready(queries, codes, lengths):
    rows, heads, group, size = queries.shape
    return pl.pallas_call(
        functools.partial(ready_kernel, codes),
        out_shape=(
            jax.ShapeDtypeStruct((heads, rows * group, 2 * size), jnp.bfloat16),
            jax.ShapeDtypeStruct((len(codes), rows, rows), jnp.bfloat16),
        ),
        in_specs=[HBM, HBM],
        out_specs=(VMEM, VMEM),
        scratch_shapes=[
            pltpu.SMEM(lengths.shape, jnp.int32),
            pltpu.VMEM(queries.shape, jnp.bfloat16),
            pltpu.SemaphoreType.DMA((2,)),
        ],
        compiler_params=PARAMS,
        name="ready",
    )(pltpu.with_memory_space_constraint(lengths, pltpu.HBM), pltpu.with_memory_space_constraint(queries, pltpu.HBM))


def stage_shapes(shape):
    return [pltpu.VMEM(shape, jnp.bfloat16), pltpu.SemaphoreType.DMA((shape[0] * shape[1] * shape[2] // min(ROW_TILE, shape[0] * shape[2]),))]


def attend_near(shape, lhs, bias, pieces):
    rows, heads, group, size = shape
    return pl.pallas_call(
        near_kernel,
        out_shape=(
            jax.ShapeDtypeStruct(shape, jnp.bfloat16),
            jax.ShapeDtypeStruct((heads, rows * group, size), jnp.float32),
            jax.ShapeDtypeStruct((heads, rows * group, 2 * size), jnp.float32),
        ),
        in_specs=[VMEM, VMEM] + [VMEM] * len(pieces),
        out_specs=(ANY, VMEM, VMEM),
        scratch_shapes=stage_shapes(shape),
        compiler_params=PARAMS,
        name="near",
    )(lhs, bias, *pieces)


def attend_middle(lhs, bias, skip, state, pieces):
    out, peak, both = state
    peak, both = pl.pallas_call(
        functools.partial(middle_kernel, skip),
        out_shape=(jax.ShapeDtypeStruct(peak.shape, peak.dtype), jax.ShapeDtypeStruct(both.shape, both.dtype)),
        in_specs=[VMEM] * (4 + len(pieces)),
        out_specs=(VMEM, VMEM),
        compiler_params=PARAMS,
        name="middle",
    )(lhs, bias, peak, both, *pieces)
    return out, peak, both


def attend_far(lhs, bias, skip, state, pieces):
    shape = state[0].shape
    return pl.pallas_call(
        functools.partial(far_kernel, skip),
        out_shape=jax.ShapeDtypeStruct(shape, jnp.bfloat16),
        in_specs=[VMEM, VMEM, ANY, VMEM, VMEM] + [VMEM] * len(pieces),
        out_specs=ANY,
        scratch_shapes=stage_shapes(shape),
        input_output_aliases={2: 0},
        compiler_params=PARAMS,
        name="far",
    )(lhs, bias, *state, *pieces)


def attend_exchanged(groups, queries, block, lengths):
    def swap(array, code, lower_code=None, flip=0):
        lower_code = code if lower_code is None else lower_code
        pairs = []
        for g in range(groups):
            for i in range(8):
                target = (g, i ^ code) if i >= 4 else (g ^ flip, i ^ lower_code)
                pairs.append((g * 8 + i, target[0] * 8 + target[1]))
        return lax.ppermute(array, ("groups", "ctx"), pairs)

    crossed = swap(block, 6)
    near = [swap(block, code) for code in (3, 2, 1)]
    lhs, bias = make_ready(queries, (0, 3, 2, 1, 6, 5, 4, 7), lengths)
    crossed, lhs = lax.optimization_barrier((crossed, lhs))
    aside = dict(lower_code=0, flip=1) if groups % 2 == 0 else dict(lower_code=1)
    spread = [swap(crossed, 3, **aside), swap(crossed, 2), swap(crossed, 1)]
    state = attend_near(queries.shape, lhs, bias, [block, *near, crossed])
    state = attend_middle(lhs, bias, 5, state, spread[:1])
    return attend_far(lhs, bias, 6, state, spread[1:])


def stream_kernel(step, lengths, query_ref, block_ref, out_ref, peak_ref, both_ref):
    rows, _, group, size = query_ref.shape
    own = lax.axis_index("ctx")
    chunk = pl.program_id(1)
    scale = math.log2(math.e) / math.sqrt(size)

    @pl.when(chunk == 0)
    def _():
        peak_ref[...] = jnp.full_like(peak_ref, MASKED)
        both_ref[...] = jnp.zeros_like(both_ref)

    low, start = jnp.int32(0), jnp.int32(0)
    for n in range(lengths.shape[0]):
        low = jnp.where(own * rows >= start, start, low)
        start = start + lengths[n]

    @pl.when((chunk * step <= own) & ((chunk + 1) * step * rows > low))
    def _():
        tile = rows * group
        query_row = lax.broadcasted_iota(jnp.int32, (tile, rows), 0) // group
        column = lax.broadcasted_iota(jnp.int32, (tile, rows), 1)
        selector = jnp.where(query_row == column, 1.0, 0.0).astype(jnp.bfloat16)
        lhs = jnp.concatenate([query_ref[:, 0].reshape(tile, size), selector], axis=1)
        rhs = jnp.concatenate(
            [
                jnp.concatenate([block_ref[b, 0, 0], key_bias(lengths, own, chunk * step + b, rows)], axis=1)
                for b in range(step)
            ],
            axis=0,
        )
        scores = lax.dot_general(lhs, rhs, (((1,), (1,)), ((), ())), preferred_element_type=jnp.float32)
        before = peak_ref[...]
        peak = jnp.maximum(before, jnp.max(scores, axis=1, keepdims=True))
        weights = jnp.exp2((scores - peak[:, :1]) * scale)
        weights = jnp.where(scores > 0.5 * MASKED, weights, 0.0).astype(jnp.bfloat16)
        value = jnp.concatenate([block_ref[b, 1, 0] for b in range(step)], axis=0)
        right = jnp.concatenate([value, jnp.ones_like(value)], axis=1)
        both_ref[...] = both_ref[...] * jnp.exp2((before[:, :1] - peak[:, :1]) * scale) + jnp.dot(
            weights, right, preferred_element_type=jnp.float32
        )
        peak_ref[...] = peak

    @pl.when(chunk == pl.num_programs(1) - 1)
    def _():
        result = both_ref[:, :size] / both_ref[:, size:]
        out_ref[:, 0] = result.astype(jnp.bfloat16).reshape(rows, group, size)


def attend_gathered(queries, blocks, lengths):
    rows, heads, group, size = queries.shape
    count = blocks.shape[0]
    step = math.gcd(count, 4)
    query_spec = pl.BlockSpec((rows, 1, group, size), lambda h, c: (0, h, 0, 0))
    return pl.pallas_call(
        functools.partial(stream_kernel, step),
        grid=(heads, count // step),
        out_shape=jax.ShapeDtypeStruct(queries.shape, jnp.bfloat16),
        in_specs=[
            pl.BlockSpec(memory_space=pltpu.SMEM),
            query_spec,
            pl.BlockSpec((step, 2, 1, rows, size), lambda h, c: (c, 0, h, 0, 0)),
        ],
        out_specs=query_spec,
        scratch_shapes=[
            pltpu.VMEM((rows * group, size), jnp.float32),
            pltpu.VMEM((rows * group, 2 * size), jnp.float32),
        ],
        compiler_params=pltpu.CompilerParams(vmem_limit_bytes=48 * 1024 * 1024),
    )(lengths, queries, blocks)


def on_device(groups, ctx, queries, keys, values, seq_lengths):
    block = jnp.stack([keys, values]).transpose(0, 2, 1, 3)
    if ctx != 8:
        return attend_gathered(queries, lax.all_gather(block, "ctx"), seq_lengths)
    return attend_exchanged(groups, queries, block, seq_lengths)


def solution(mesh):
    placed = (
        P(("groups", "ctx"), "kvh", None, None),
        P(("groups", "ctx"), "kvh", None),
        P(("groups", "ctx"), "kvh", None),
        P("groups"),
    )
    return jax.shard_map(
        functools.partial(on_device, mesh.shape["groups"], mesh.shape["ctx"]),
        mesh=mesh,
        in_specs=placed,
        out_specs=P(("groups", "ctx"), "kvh", None, None),
        check_vma=False,
    )
```

```python
import functools
import math

import jax
import jax.numpy as jnp
from jax import lax
from jax.experimental import pallas as pl
from jax.experimental.pallas import tpu as pltpu
from jax.sharding import PartitionSpec as P

MASKED = -1e30
ROW_TILE = 256
HEADROOM = 60.0


def key_bias(lengths, own, block, rows):
    key_pos = block * rows + lax.broadcasted_iota(jnp.int32, (rows, rows), 0)
    query_pos = own * rows + lax.broadcasted_iota(jnp.int32, (rows, rows), 1)
    low = jnp.zeros((rows, rows), jnp.int32)
    start = jnp.int32(0)
    for n in range(lengths.shape[0]):
        low = jnp.where(query_pos >= start, start, low)
        start = start + lengths[n]
    allowed = (key_pos >= low) & (key_pos <= query_pos)
    return jnp.where(allowed, 0.0, MASKED).astype(jnp.bfloat16)


def ready_kernel(codes, lengths_hbm, query_hbm, lhs_ref, bias_ref, lengths, query_ref, semaphores):
    rows, heads, group, size = query_ref.shape
    fetches = [
        pltpu.make_async_copy(lengths_hbm, lengths, semaphores.at[0]),
        pltpu.make_async_copy(query_hbm, query_ref, semaphores.at[1]),
    ]
    for fetch in fetches:
        fetch.start()
    own = lax.axis_index("ctx")
    query_row = lax.broadcasted_iota(jnp.int32, (rows * group, rows), 0) // group
    column = lax.broadcasted_iota(jnp.int32, (rows * group, rows), 1)
    selector = jnp.where(query_row == column, 1.0, 0.0).astype(jnp.bfloat16)
    for h in range(heads):
        lhs_ref[h, :, size:] = selector
    fetches[0].wait()
    for n, code in enumerate(codes):
        bias_ref[n] = key_bias(lengths, own, own ^ code, rows)
    fetches[1].wait()
    for h in range(heads):
        lhs_ref[h, :, :size] = query_ref[:, h].reshape(rows * group, size)


def scores_of(lhs, h, pieces, biases):
    rhs = jnp.concatenate([jnp.concatenate([p[0, h], b], axis=1) for p, b in zip(pieces, biases)], axis=0)
    return lax.dot_general(lhs, rhs, (((1,), (1,)), ((), ())), preferred_element_type=jnp.float32)


def weigh(above, h, pieces):
    weights = jnp.exp2(above).astype(jnp.bfloat16)
    ones = jnp.ones_like(pieces[0][1, h])
    right = jnp.concatenate([jnp.concatenate([p[1, h], ones], axis=1) for p in pieces], axis=0)
    return jnp.dot(weights, right, preferred_element_type=jnp.float32)


class State:
    def __init__(self, peak_ref, both_ref):
        self.peak, self.both = peak_ref, both_ref

    def restart(self):
        pass

    def wait(self):
        pass

    def __call__(self, h, first, peak, both):
        rows = pl.ds(first, both.shape[0])
        self.peak[h, rows] = jnp.broadcast_to(peak, (both.shape[0], self.peak.shape[-1]))
        self.both[h, rows] = both


class Output:
    def __init__(self, out_ref, stage_ref, semaphores):
        self.out, self.stage, self.semaphores, self.copies = out_ref, stage_ref, semaphores, []

    def restart(self):
        self.copies = []

    def wait(self):
        for copy in self.copies:
            copy.wait()

    def __call__(self, h, first, peak, both):
        _, _, group, size = self.stage.shape
        result = both[:, :size] / both[:, size:]
        queries = pl.ds(first // group, result.shape[0] // group)
        self.stage[queries, h] = result.astype(jnp.bfloat16).reshape(-1, group, size)
        copy = pltpu.make_async_copy(
            self.stage.at[queries, h], self.out.at[queries, h], self.semaphores.at[len(self.copies)]
        )
        copy.start()
        self.copies.append(copy)


def tiles_of(lhs_ref):
    heads, rows, _ = lhs_ref.shape
    tile = min(ROW_TILE, rows)
    return [(h, first, tile) for first in range(0, rows, tile) for h in range(heads)]


def near_kernel(lhs_ref, bias_ref, *refs):
    pieces, (out_ref, peak_ref, both_ref, stage_ref, semaphores) = refs[:-5], refs[-5:]
    size = stage_ref.shape[-1]
    scale = math.log2(math.e) / math.sqrt(size)
    upper = lax.axis_index("ctx") >= 4
    biases = [bias_ref[n] for n in range(len(pieces))]

    def attend(members, put):
        for h, first, tile in tiles_of(lhs_ref):
            scores = scores_of(lhs_ref[h, pl.ds(first, tile)], h, members, biases)
            peak = jnp.max(scores, axis=1, keepdims=True)
            put(h, first, peak, weigh((scores - peak) * scale, h, members))
        put.wait()

    @pl.when(upper)
    def _():
        attend(pieces, State(peak_ref, both_ref))

    @pl.when(jnp.logical_not(upper))
    def _():
        attend(pieces[:4], Output(out_ref, stage_ref, semaphores))


def fold(lhs_ref, peak_ref, both_ref, pieces, biases, put):
    size = peak_ref.shape[-1]
    scale = math.log2(math.e) / math.sqrt(size)
    most = jnp.full((1, 1), MASKED, jnp.float32)
    for h, first, tile in tiles_of(lhs_ref):
        rows = pl.ds(first, tile)
        before = peak_ref[h, rows]
        scores = scores_of(lhs_ref[h, rows], h, pieces, biases)
        above = (scores - jnp.concatenate([before] * len(pieces), axis=1)) * scale
        most = jnp.maximum(most, jnp.max(above, axis=0, keepdims=True))
        put(h, first, before, both_ref[h, rows] + weigh(above, h, pieces))
    put.wait()

    @pl.when(jnp.max(most) > HEADROOM)
    def _():
        put.restart()
        for h, first, tile in tiles_of(lhs_ref):
            rows = pl.ds(first, tile)
            scores = scores_of(lhs_ref[h, rows], h, pieces, biases)
            before = peak_ref[h, rows]
            peak = jnp.maximum(before, jnp.max(scores, axis=1, keepdims=True))
            fade = jnp.exp2((before - peak) * scale)
            added = weigh((scores - jnp.concatenate([peak] * len(pieces), axis=1)) * scale, h, pieces)
            put(h, first, peak, both_ref[h, rows] * jnp.concatenate([fade, fade], axis=1) + added)
        put.wait()


def middle_kernel(skip, lhs_ref, bias_ref, peak_ref, both_ref, *refs):
    pieces, (peak_out, both_out) = refs[:-2], refs[-2:]
    biases = [bias_ref[skip + n] for n in range(len(pieces))]

    @pl.when(lax.axis_index("ctx") >= 4)
    def _():
        fold(lhs_ref, peak_ref, both_ref, pieces, biases, State(peak_out, both_out))


def far_kernel(skip, lhs_ref, bias_ref, _, peak_ref, both_ref, *refs):
    pieces, (out_ref, stage_ref, semaphores) = refs[:-3], refs[-3:]
    biases = [bias_ref[skip + n] for n in range(len(pieces))]

    @pl.when(lax.axis_index("ctx") >= 4)
    def _():
        fold(lhs_ref, peak_ref, both_ref, pieces, biases, Output(out_ref, stage_ref, semaphores))


VMEM = pl.BlockSpec(memory_space=pltpu.VMEM)
ANY = pl.BlockSpec(memory_space=pl.ANY)
HBM = pl.BlockSpec(memory_space=pltpu.HBM)
PARAMS = pltpu.CompilerParams(vmem_limit_bytes=24 * 1024 * 1024)


def make_ready(queries, codes, lengths):
    rows, heads, group, size = queries.shape
    return pl.pallas_call(
        functools.partial(ready_kernel, codes),
        out_shape=(
            jax.ShapeDtypeStruct((heads, rows * group, 2 * size), jnp.bfloat16),
            jax.ShapeDtypeStruct((len(codes), rows, rows), jnp.bfloat16),
        ),
        in_specs=[HBM, HBM],
        out_specs=(VMEM, VMEM),
        scratch_shapes=[
            pltpu.SMEM(lengths.shape, jnp.int32),
            pltpu.VMEM(queries.shape, jnp.bfloat16),
            pltpu.SemaphoreType.DMA((2,)),
        ],
        compiler_params=PARAMS,
        name="ready",
    )(pltpu.with_memory_space_constraint(lengths, pltpu.HBM), pltpu.with_memory_space_constraint(queries, pltpu.HBM))


def stage_shapes(shape):
    return [pltpu.VMEM(shape, jnp.bfloat16), pltpu.SemaphoreType.DMA((shape[0] * shape[1] * shape[2] // min(ROW_TILE, shape[0] * shape[2]),))]


def attend_near(shape, lhs, bias, pieces):
    rows, heads, group, size = shape
    return pl.pallas_call(
        near_kernel,
        out_shape=(
            jax.ShapeDtypeStruct(shape, jnp.bfloat16),
            jax.ShapeDtypeStruct((heads, rows * group, size), jnp.float32),
            jax.ShapeDtypeStruct((heads, rows * group, 2 * size), jnp.float32),
        ),
        in_specs=[VMEM, VMEM] + [VMEM] * len(pieces),
        out_specs=(ANY, VMEM, VMEM),
        scratch_shapes=stage_shapes(shape),
        compiler_params=PARAMS,
        name="near",
    )(lhs, bias, *pieces)


def attend_middle(lhs, bias, skip, state, pieces):
    out, peak, both = state
    peak, both = pl.pallas_call(
        functools.partial(middle_kernel, skip),
        out_shape=(jax.ShapeDtypeStruct(peak.shape, peak.dtype), jax.ShapeDtypeStruct(both.shape, both.dtype)),
        in_specs=[VMEM] * (4 + len(pieces)),
        out_specs=(VMEM, VMEM),
        compiler_params=PARAMS,
        name="middle",
    )(lhs, bias, peak, both, *pieces)
    return out, peak, both


def attend_far(lhs, bias, skip, state, pieces):
    shape = state[0].shape
    return pl.pallas_call(
        functools.partial(far_kernel, skip),
        out_shape=jax.ShapeDtypeStruct(shape, jnp.bfloat16),
        in_specs=[VMEM, VMEM, ANY, VMEM, VMEM] + [VMEM] * len(pieces),
        out_specs=ANY,
        scratch_shapes=stage_shapes(shape),
        input_output_aliases={2: 0},
        compiler_params=PARAMS,
        name="far",
    )(lhs, bias, *state, *pieces)


def attend_exchanged(groups, queries, block, lengths):
    def swap(array, code, lower_code=None, flip=0):
        lower_code = code if lower_code is None else lower_code
        pairs = []
        for g in range(groups):
            for i in range(8):
                target = (g, i ^ code) if i >= 4 else (g ^ flip, i ^ lower_code)
                pairs.append((g * 8 + i, target[0] * 8 + target[1]))
        return lax.ppermute(array, ("groups", "ctx"), pairs)

    diagonal = [(g * 8 + i, g * 8 + t) for g in range(groups) for i, t in enumerate((3, 2, 0, 1, 7, 6, 4, 5))]
    crossed = swap(block, 6)
    near = [swap(block, 2), lax.ppermute(block, ("groups", "ctx"), diagonal), swap(block, 1)]
    lhs, bias = make_ready(queries, (0, 2, 3, 1, 6, 5, 4, 7), lengths)
    crossed, lhs = lax.optimization_barrier((crossed, lhs))
    aside = dict(lower_code=0, flip=1) if groups % 2 == 0 else dict(lower_code=1)
    spread = [swap(crossed, 3, **aside), swap(crossed, 2, **aside), swap(crossed, 1)]
    state = attend_near(queries.shape, lhs, bias, [block, *near, crossed])
    state = attend_middle(lhs, bias, 5, state, spread[:1])
    return attend_far(lhs, bias, 6, state, spread[1:])


def stream_kernel(step, lengths, query_ref, block_ref, out_ref, peak_ref, both_ref):
    rows, _, group, size = query_ref.shape
    own = lax.axis_index("ctx")
    chunk = pl.program_id(1)
    scale = math.log2(math.e) / math.sqrt(size)

    @pl.when(chunk == 0)
    def _():
        peak_ref[...] = jnp.full_like(peak_ref, MASKED)
        both_ref[...] = jnp.zeros_like(both_ref)

    low, start = jnp.int32(0), jnp.int32(0)
    for n in range(lengths.shape[0]):
        low = jnp.where(own * rows >= start, start, low)
        start = start + lengths[n]

    @pl.when((chunk * step <= own) & ((chunk + 1) * step * rows > low))
    def _():
        tile = rows * group
        query_row = lax.broadcasted_iota(jnp.int32, (tile, rows), 0) // group
        column = lax.broadcasted_iota(jnp.int32, (tile, rows), 1)
        selector = jnp.where(query_row == column, 1.0, 0.0).astype(jnp.bfloat16)
        lhs = jnp.concatenate([query_ref[:, 0].reshape(tile, size), selector], axis=1)
        rhs = jnp.concatenate(
            [
                jnp.concatenate([block_ref[b, 0, 0], key_bias(lengths, own, chunk * step + b, rows)], axis=1)
                for b in range(step)
            ],
            axis=0,
        )
        scores = lax.dot_general(lhs, rhs, (((1,), (1,)), ((), ())), preferred_element_type=jnp.float32)
        before = peak_ref[...]
        peak = jnp.maximum(before, jnp.max(scores, axis=1, keepdims=True))
        weights = jnp.exp2((scores - peak[:, :1]) * scale)
        weights = jnp.where(scores > 0.5 * MASKED, weights, 0.0).astype(jnp.bfloat16)
        value = jnp.concatenate([block_ref[b, 1, 0] for b in range(step)], axis=0)
        right = jnp.concatenate([value, jnp.ones_like(value)], axis=1)
        both_ref[...] = both_ref[...] * jnp.exp2((before[:, :1] - peak[:, :1]) * scale) + jnp.dot(
            weights, right, preferred_element_type=jnp.float32
        )
        peak_ref[...] = peak

    @pl.when(chunk == pl.num_programs(1) - 1)
    def _():
        result = both_ref[:, :size] / both_ref[:, size:]
        out_ref[:, 0] = result.astype(jnp.bfloat16).reshape(rows, group, size)


def attend_gathered(queries, blocks, lengths):
    rows, heads, group, size = queries.shape
    count = blocks.shape[0]
    step = math.gcd(count, 4)
    query_spec = pl.BlockSpec((rows, 1, group, size), lambda h, c: (0, h, 0, 0))
    return pl.pallas_call(
        functools.partial(stream_kernel, step),
        grid=(heads, count // step),
        out_shape=jax.ShapeDtypeStruct(queries.shape, jnp.bfloat16),
        in_specs=[
            pl.BlockSpec(memory_space=pltpu.SMEM),
            query_spec,
            pl.BlockSpec((step, 2, 1, rows, size), lambda h, c: (c, 0, h, 0, 0)),
        ],
        out_specs=query_spec,
        scratch_shapes=[
            pltpu.VMEM((rows * group, size), jnp.float32),
            pltpu.VMEM((rows * group, 2 * size), jnp.float32),
        ],
        compiler_params=pltpu.CompilerParams(vmem_limit_bytes=48 * 1024 * 1024),
    )(lengths, queries, blocks)


def on_device(groups, ctx, queries, keys, values, seq_lengths):
    block = jnp.stack([keys, values]).transpose(0, 2, 1, 3)
    if ctx != 8:
        return attend_gathered(queries, lax.all_gather(block, "ctx"), seq_lengths)
    return attend_exchanged(groups, queries, block, seq_lengths)


def solution(mesh):
    placed = (
        P(("groups", "ctx"), "kvh", None, None),
        P(("groups", "ctx"), "kvh", None),
        P(("groups", "ctx"), "kvh", None),
        P("groups"),
    )
    return jax.shard_map(
        functools.partial(on_device, mesh.shape["groups"], mesh.shape["ctx"]),
        mesh=mesh,
        in_specs=placed,
        out_specs=P(("groups", "ctx"), "kvh", None, None),
        check_vma=False,
    )
```

```python
import functools
import math

import jax
import jax.numpy as jnp
from jax import lax
from jax.experimental import pallas as pl
from jax.experimental.pallas import tpu as pltpu
from jax.sharding import PartitionSpec as P

MASKED = -1e30
ROW_TILE = 256
HEADROOM = 60.0


def key_bias(lengths, own, block, rows):
    key_pos = block * rows + lax.broadcasted_iota(jnp.int32, (rows, rows), 0)
    query_pos = own * rows + lax.broadcasted_iota(jnp.int32, (rows, rows), 1)
    low = jnp.zeros((rows, rows), jnp.int32)
    start = jnp.int32(0)
    for n in range(lengths.shape[0]):
        low = jnp.where(query_pos >= start, start, low)
        start = start + lengths[n]
    allowed = (key_pos >= low) & (key_pos <= query_pos)
    return jnp.where(allowed, 0.0, MASKED).astype(jnp.bfloat16)


def ready_kernel(codes, lengths_hbm, query_hbm, lhs_ref, bias_ref, lengths, query_ref, semaphores):
    rows, heads, group, size = query_ref.shape
    fetches = [
        pltpu.make_async_copy(lengths_hbm, lengths, semaphores.at[0]),
        pltpu.make_async_copy(query_hbm, query_ref, semaphores.at[1]),
    ]
    for fetch in fetches:
        fetch.start()
    own = lax.axis_index("ctx")
    query_row = lax.broadcasted_iota(jnp.int32, (rows * group, rows), 0) // group
    column = lax.broadcasted_iota(jnp.int32, (rows * group, rows), 1)
    selector = jnp.where(query_row == column, 1.0, 0.0).astype(jnp.bfloat16)
    for h in range(heads):
        lhs_ref[h, :, size:] = selector
    fetches[0].wait()
    for n, code in enumerate(codes):
        bias_ref[n] = key_bias(lengths, own, own ^ code, rows)
    fetches[1].wait()
    for h in range(heads):
        lhs_ref[h, :, :size] = query_ref[:, h].reshape(rows * group, size)


def scores_of(lhs, h, pieces, biases):
    rhs = jnp.concatenate([jnp.concatenate([p[0, h], b], axis=1) for p, b in zip(pieces, biases)], axis=0)
    return lax.dot_general(lhs, rhs, (((1,), (1,)), ((), ())), preferred_element_type=jnp.float32)


def weigh(above, h, pieces):
    weights = jnp.exp2(above).astype(jnp.bfloat16)
    ones = jnp.ones_like(pieces[0][1, h])
    right = jnp.concatenate([jnp.concatenate([p[1, h], ones], axis=1) for p in pieces], axis=0)
    return jnp.dot(weights, right, preferred_element_type=jnp.float32)


class State:
    def __init__(self, peak_ref, both_ref):
        self.peak, self.both = peak_ref, both_ref

    def restart(self):
        pass

    def wait(self):
        pass

    def __call__(self, h, first, peak, both):
        rows = pl.ds(first, both.shape[0])
        self.peak[h, rows] = jnp.broadcast_to(peak, (both.shape[0], self.peak.shape[-1]))
        self.both[h, rows] = both


class Output:
    def __init__(self, out_ref, stage_ref, semaphores):
        self.out, self.stage, self.semaphores, self.copies = out_ref, stage_ref, semaphores, []

    def restart(self):
        self.copies = []

    def wait(self):
        for copy in self.copies:
            copy.wait()

    def __call__(self, h, first, peak, both):
        _, _, group, size = self.stage.shape
        result = both[:, :size] / both[:, size:]
        queries = pl.ds(first // group, result.shape[0] // group)
        self.stage[queries, h] = result.astype(jnp.bfloat16).reshape(-1, group, size)
        copy = pltpu.make_async_copy(
            self.stage.at[queries, h], self.out.at[queries, h], self.semaphores.at[len(self.copies)]
        )
        copy.start()
        self.copies.append(copy)


def tiles_of(lhs_ref):
    heads, rows, _ = lhs_ref.shape
    tile = min(ROW_TILE, rows)
    return [(h, first, tile) for first in range(0, rows, tile) for h in range(heads)]


def near_kernel(lhs_ref, bias_ref, *refs):
    pieces, (out_ref, peak_ref, both_ref, stage_ref, semaphores) = refs[:-5], refs[-5:]
    size = stage_ref.shape[-1]
    scale = math.log2(math.e) / math.sqrt(size)
    upper = lax.axis_index("ctx") >= 4
    biases = [bias_ref[n] for n in range(len(pieces))]

    def attend(members, put):
        for h, first, tile in tiles_of(lhs_ref):
            scores = scores_of(lhs_ref[h, pl.ds(first, tile)], h, members, biases)
            peak = jnp.max(scores, axis=1, keepdims=True)
            put(h, first, peak, weigh((scores - peak) * scale, h, members))
        put.wait()

    @pl.when(upper)
    def _():
        attend(pieces, State(peak_ref, both_ref))

    @pl.when(jnp.logical_not(upper))
    def _():
        attend(pieces[:4], Output(out_ref, stage_ref, semaphores))


def fold(lhs_ref, peak_ref, both_ref, pieces, biases, put):
    size = peak_ref.shape[-1]
    scale = math.log2(math.e) / math.sqrt(size)
    most = jnp.full((1, 1), MASKED, jnp.float32)
    for h, first, tile in tiles_of(lhs_ref):
        rows = pl.ds(first, tile)
        before = peak_ref[h, rows]
        scores = scores_of(lhs_ref[h, rows], h, pieces, biases)
        above = (scores - jnp.concatenate([before] * len(pieces), axis=1)) * scale
        most = jnp.maximum(most, jnp.max(above, axis=0, keepdims=True))
        put(h, first, before, both_ref[h, rows] + weigh(above, h, pieces))
    put.wait()

    @pl.when(jnp.max(most) > HEADROOM)
    def _():
        put.restart()
        for h, first, tile in tiles_of(lhs_ref):
            rows = pl.ds(first, tile)
            scores = scores_of(lhs_ref[h, rows], h, pieces, biases)
            before = peak_ref[h, rows]
            peak = jnp.maximum(before, jnp.max(scores, axis=1, keepdims=True))
            fade = jnp.exp2((before - peak) * scale)
            added = weigh((scores - jnp.concatenate([peak] * len(pieces), axis=1)) * scale, h, pieces)
            put(h, first, peak, both_ref[h, rows] * jnp.concatenate([fade, fade], axis=1) + added)
        put.wait()


def middle_kernel(skip, lhs_ref, bias_ref, peak_ref, both_ref, *refs):
    pieces, (peak_out, both_out) = refs[:-2], refs[-2:]
    biases = [bias_ref[skip + n] for n in range(len(pieces))]

    @pl.when(lax.axis_index("ctx") >= 4)
    def _():
        fold(lhs_ref, peak_ref, both_ref, pieces, biases, State(peak_out, both_out))


def far_kernel(skip, lhs_ref, bias_ref, _, peak_ref, both_ref, *refs):
    pieces, (out_ref, stage_ref, semaphores) = refs[:-3], refs[-3:]
    biases = [bias_ref[skip + n] for n in range(len(pieces))]

    @pl.when(lax.axis_index("ctx") >= 4)
    def _():
        fold(lhs_ref, peak_ref, both_ref, pieces, biases, Output(out_ref, stage_ref, semaphores))


VMEM = pl.BlockSpec(memory_space=pltpu.VMEM)
ANY = pl.BlockSpec(memory_space=pl.ANY)
HBM = pl.BlockSpec(memory_space=pltpu.HBM)
PARAMS = pltpu.CompilerParams(vmem_limit_bytes=24 * 1024 * 1024)


def make_ready(queries, codes, lengths):
    rows, heads, group, size = queries.shape
    return pl.pallas_call(
        functools.partial(ready_kernel, codes),
        out_shape=(
            jax.ShapeDtypeStruct((heads, rows * group, 2 * size), jnp.bfloat16),
            jax.ShapeDtypeStruct((len(codes), rows, rows), jnp.bfloat16),
        ),
        in_specs=[HBM, HBM],
        out_specs=(VMEM, VMEM),
        scratch_shapes=[
            pltpu.SMEM(lengths.shape, jnp.int32),
            pltpu.VMEM(queries.shape, jnp.bfloat16),
            pltpu.SemaphoreType.DMA((2,)),
        ],
        compiler_params=PARAMS,
        name="ready",
    )(pltpu.with_memory_space_constraint(lengths, pltpu.HBM), pltpu.with_memory_space_constraint(queries, pltpu.HBM))


def stage_shapes(shape):
    return [pltpu.VMEM(shape, jnp.bfloat16), pltpu.SemaphoreType.DMA((shape[0] * shape[1] * shape[2] // min(ROW_TILE, shape[0] * shape[2]),))]


def attend_near(shape, lhs, bias, pieces):
    rows, heads, group, size = shape
    return pl.pallas_call(
        near_kernel,
        out_shape=(
            jax.ShapeDtypeStruct(shape, jnp.bfloat16),
            jax.ShapeDtypeStruct((heads, rows * group, size), jnp.float32),
            jax.ShapeDtypeStruct((heads, rows * group, 2 * size), jnp.float32),
        ),
        in_specs=[VMEM, VMEM] + [VMEM] * len(pieces),
        out_specs=(ANY, VMEM, VMEM),
        scratch_shapes=stage_shapes(shape),
        compiler_params=PARAMS,
        name="near",
    )(lhs, bias, *pieces)


def attend_middle(lhs, bias, skip, state, pieces):
    out, peak, both = state
    peak, both = pl.pallas_call(
        functools.partial(middle_kernel, skip),
        out_shape=(jax.ShapeDtypeStruct(peak.shape, peak.dtype), jax.ShapeDtypeStruct(both.shape, both.dtype)),
        in_specs=[VMEM] * (4 + len(pieces)),
        out_specs=(VMEM, VMEM),
        compiler_params=PARAMS,
        name="middle",
    )(lhs, bias, peak, both, *pieces)
    return out, peak, both


def attend_far(lhs, bias, skip, state, pieces):
    shape = state[0].shape
    return pl.pallas_call(
        functools.partial(far_kernel, skip),
        out_shape=jax.ShapeDtypeStruct(shape, jnp.bfloat16),
        in_specs=[VMEM, VMEM, ANY, VMEM, VMEM] + [VMEM] * len(pieces),
        out_specs=ANY,
        scratch_shapes=stage_shapes(shape),
        input_output_aliases={2: 0},
        compiler_params=PARAMS,
        name="far",
    )(lhs, bias, *state, *pieces)


def attend_exchanged(groups, queries, block, lengths):
    def swap(array, code, lower_code=None, flip=0):
        lower_code = code if lower_code is None else lower_code
        pairs = []
        for g in range(groups):
            for i in range(8):
                target = (g, i ^ code) if i >= 4 else (g ^ flip, i ^ lower_code)
                pairs.append((g * 8 + i, target[0] * 8 + target[1]))
        return lax.ppermute(array, ("groups", "ctx"), pairs)

    crossed = swap(block, 6)
    near = [swap(block, code) for code in (3, 2, 1)]
    lhs, bias = make_ready(queries, (0, 3, 2, 1, 6, 7, 5, 4), lengths)
    crossed, lhs = lax.optimization_barrier((crossed, lhs))
    aside = dict(lower_code=0, flip=1) if groups % 2 == 0 else dict(lower_code=1)
    spread = [swap(crossed, 3, **aside), swap(crossed, 2), swap(crossed, 1)]
    state = attend_near(queries.shape, lhs, bias, [block, *near, crossed])
    state = attend_middle(lhs, bias, 5, state, spread[2:])
    return attend_far(lhs, bias, 6, state, spread[:2])


def stream_kernel(step, lengths, query_ref, block_ref, out_ref, peak_ref, both_ref):
    rows, _, group, size = query_ref.shape
    own = lax.axis_index("ctx")
    chunk = pl.program_id(1)
    scale = math.log2(math.e) / math.sqrt(size)

    @pl.when(chunk == 0)
    def _():
        peak_ref[...] = jnp.full_like(peak_ref, MASKED)
        both_ref[...] = jnp.zeros_like(both_ref)

    low, start = jnp.int32(0), jnp.int32(0)
    for n in range(lengths.shape[0]):
        low = jnp.where(own * rows >= start, start, low)
        start = start + lengths[n]

    @pl.when((chunk * step <= own) & ((chunk + 1) * step * rows > low))
    def _():
        tile = rows * group
        query_row = lax.broadcasted_iota(jnp.int32, (tile, rows), 0) // group
        column = lax.broadcasted_iota(jnp.int32, (tile, rows), 1)
        selector = jnp.where(query_row == column, 1.0, 0.0).astype(jnp.bfloat16)
        lhs = jnp.concatenate([query_ref[:, 0].reshape(tile, size), selector], axis=1)
        rhs = jnp.concatenate(
            [
                jnp.concatenate([block_ref[b, 0, 0], key_bias(lengths, own, chunk * step + b, rows)], axis=1)
                for b in range(step)
            ],
            axis=0,
        )
        scores = lax.dot_general(lhs, rhs, (((1,), (1,)), ((), ())), preferred_element_type=jnp.float32)
        before = peak_ref[...]
        peak = jnp.maximum(before, jnp.max(scores, axis=1, keepdims=True))
        weights = jnp.exp2((scores - peak[:, :1]) * scale)
        weights = jnp.where(scores > 0.5 * MASKED, weights, 0.0).astype(jnp.bfloat16)
        value = jnp.concatenate([block_ref[b, 1, 0] for b in range(step)], axis=0)
        right = jnp.concatenate([value, jnp.ones_like(value)], axis=1)
        both_ref[...] = both_ref[...] * jnp.exp2((before[:, :1] - peak[:, :1]) * scale) + jnp.dot(
            weights, right, preferred_element_type=jnp.float32
        )
        peak_ref[...] = peak

    @pl.when(chunk == pl.num_programs(1) - 1)
    def _():
        result = both_ref[:, :size] / both_ref[:, size:]
        out_ref[:, 0] = result.astype(jnp.bfloat16).reshape(rows, group, size)


def attend_gathered(queries, blocks, lengths):
    rows, heads, group, size = queries.shape
    count = blocks.shape[0]
    step = math.gcd(count, 4)
    query_spec = pl.BlockSpec((rows, 1, group, size), lambda h, c: (0, h, 0, 0))
    return pl.pallas_call(
        functools.partial(stream_kernel, step),
        grid=(heads, count // step),
        out_shape=jax.ShapeDtypeStruct(queries.shape, jnp.bfloat16),
        in_specs=[
            pl.BlockSpec(memory_space=pltpu.SMEM),
            query_spec,
            pl.BlockSpec((step, 2, 1, rows, size), lambda h, c: (c, 0, h, 0, 0)),
        ],
        out_specs=query_spec,
        scratch_shapes=[
            pltpu.VMEM((rows * group, size), jnp.float32),
            pltpu.VMEM((rows * group, 2 * size), jnp.float32),
        ],
        compiler_params=pltpu.CompilerParams(vmem_limit_bytes=48 * 1024 * 1024),
    )(lengths, queries, blocks)


def on_device(groups, ctx, queries, keys, values, seq_lengths):
    block = jnp.stack([keys, values]).transpose(0, 2, 1, 3)
    if ctx != 8:
        return attend_gathered(queries, lax.all_gather(block, "ctx"), seq_lengths)
    return attend_exchanged(groups, queries, block, seq_lengths)


def solution(mesh):
    placed = (
        P(("groups", "ctx"), "kvh", None, None),
        P(("groups", "ctx"), "kvh", None),
        P(("groups", "ctx"), "kvh", None),
        P("groups"),
    )
    return jax.shard_map(
        functools.partial(on_device, mesh.shape["groups"], mesh.shape["ctx"]),
        mesh=mesh,
        in_specs=placed,
        out_specs=P(("groups", "ctx"), "kvh", None, None),
        check_vma=False,
    )
```
